32 devices in a mesh: row: 4 (over y, x), col: 8 (over z, core).
Axes of the slice: x: 2, y: 2, z: 4, core: 2. Of those that a mesh axis runs over, the one named last changes fastest.
Arguments:
- features: bfloat16 [32768, 128], P(('row', 'col')), may hold values from -6 to 6
- pair_index: int32 [2, 4096], P(None, ('row', 'col')), may hold values from -1 to 63, as said below
- bins: int32 [4096, 128, 128], P(('row', 'col')), may hold values from 0 to 8, as said below
- plate_weight: bfloat16 [1024, 128], replicated, may hold values from -0.1875 to 0.1875
- tower_weight: bfloat16 [1024, 128], replicated, may hold values from -0.1875 to 0.1875
- norm_gain: float32 [128], replicated, may hold values from 0.1 to 1.9
- update_in: bfloat16 [256, 128], replicated, may hold values from -0.375 to 0.375
- update_out: bfloat16 [128, 128], replicated, may hold values from -0.5 to 0.5
Outputs:
- updated: bfloat16 [32768, 128], P(('row', 'col'))
The draws below stay inside these ranges and needn't reach their ends.
Inputs may be any that keep to these rules, and one draw needn't show every extreme that they name: `pair_index`: row 0 is a cluster of the meeting device's plate (below 64), row 1 a cluster of its tower (below 32). The 128 slots of one meeting device hold its live pairs first and then -1 in both rows. No cluster pair is live twice on one device. Some device has all 128 slots live. `bins`: 8 marks an atom pair that is no neighbour.
All inputs are finite; a program needn't handle non-finite values.
Results may differ from the reference program's by a relative error of at most 0.008.
Values may be sent and summed in bfloat16 or wider, within the bound.
A program may use at most 128 MiB of HBM per device.

```python
import jax
import jax.numpy as jnp
from jax import lax

D = 128
CLUSTER = 128
BINS = 8
HOME_DEV = 8
PAIRS_DEV = 128
PLATE = 64
TOWER = 32
CLUSTERS = 256
N_ROW = 4
N_COL = 8


def draw_pair_index(key, part):
    devices = N_ROW * N_COL
    keys = jax.random.split(jax.random.fold_in(key, 11), devices)
    lowest = max(1, PAIRS_DEV // 8)

    def one_device(inner):
        first, second, third = jax.random.split(inner, 3)
        codes = jax.random.permutation(first, PLATE * TOWER)[:PAIRS_DEV]
        heavy = jax.random.randint(second, (), 0, 6) == 0
        light = jax.random.randint(third, (), lowest, PAIRS_DEV // 3 + 1)
        return (codes, jnp.where(heavy, PAIRS_DEV, light))
    codes, counts = jax.vmap(one_device)(keys)
    forced = jax.random.randint(jax.random.fold_in(key, 12), (), 0, devices)
    counts = jnp.where(jnp.arange(devices) == forced, PAIRS_DEV, counts)
    live = jnp.arange(PAIRS_DEV)[None, :] < counts[:, None]
    plate_idx = jnp.where(live, codes // TOWER, -1)
    tower_idx = jnp.where(live, codes % TOWER, -1)
    return jnp.stack([plate_idx.reshape(-1), tower_idx.reshape(-1)]).astype(jnp.int32)


def draw_bins(key, part):
    total = PAIRS_DEV * N_ROW * N_COL
    raw = jax.random.randint(jax.random.fold_in(key, 21), (total, CLUSTER, CLUSTER), 0, 3 * BINS)
    return jnp.where(raw < BINS, raw, BINS).astype(jnp.int32)


def level_of(rng, dims, cuts, smallest, top_value):
    gain, own = 1.0, jax.random.fold_in(rng, 6)
    for axis_at, parts in cuts:
        heights = jnp.exp(jax.random.uniform(jax.random.fold_in(own, axis_at), (parts,), jnp.float32, smallest / len(cuts), top_value / len(cuts)))
        gain = gain * jnp.repeat(heights, dims[axis_at] // parts).reshape([-1 if axis == axis_at else 1 for axis in range(len(dims))])
    return gain


def scatter_about(stream_key, dims, width, reach, cuts=(), kind=jnp.bfloat16):
    entries = jax.random.normal(stream_key, dims, jnp.float32) * width
    if len(cuts) > 0:
        entries = level_of(stream_key, dims, cuts, -0.22, 0.18) * entries
    return jnp.clip(entries, min=-reach, max=reach).astype(kind)


def setup_inputs(seed: int = 0) -> dict:
    splits = jax.random.split(jax.random.key(seed), 9)
    features = scatter_about(splits[0], (CLUSTERS * CLUSTER, D), 1.0, 6.0, ((0, 32),))
    pair_index = draw_pair_index(jax.random.fold_in(splits[8], 71), 0)
    bins = draw_bins(jax.random.fold_in(splits[8], 71), 0)
    plate_weight = scatter_about(splits[3], (BINS * D, D), (BINS * D) ** -0.5, 0.1875)
    tower_weight = scatter_about(splits[4], (BINS * D, D), (BINS * D) ** -0.5, 0.1875)
    norm_gain = jnp.clip(1.0 + 0.18 * jax.random.normal(splits[5], (D,), jnp.float32), 0.1, 1.9)
    update_in = scatter_about(splits[6], (2 * D, D), (2 * D) ** -0.5, 0.375)
    update_out = scatter_about(splits[7], (D, D), D ** -0.5, 0.5)
    return {"features": features, "pair_index": pair_index, "bins": bins, "plate_weight": plate_weight, "tower_weight": tower_weight, "norm_gain": norm_gain, "update_in": update_in, "update_out": update_out}


def pair_messages(plate, tower, plate_idx, tower_idx, block, plate_weight, tower_weight):
    live = plate_idx >= 0
    plate_at = jnp.maximum(plate_idx, 0).astype(jnp.int32)
    tower_at = jnp.maximum(tower_idx, 0).astype(jnp.int32)
    levels = jnp.arange(BINS, dtype=jnp.int32)
    basis = ((block[:, :, None, :] == levels[None, None, :, None]) & live[:, None, None, None]).astype(jnp.float32)
    far_side = tower[tower_at].astype(jnp.float32)
    near_side = plate[plate_at].astype(jnp.float32)
    near_plate = jnp.einsum('gakb,gbd->gakd', basis, far_side).astype(jnp.bfloat16)
    near_tower = jnp.einsum('gakb,gad->gbkd', basis, near_side).astype(jnp.bfloat16)
    count = block.shape[0]
    to_plate = jnp.dot(near_plate.reshape(count * CLUSTER, BINS * D), plate_weight, preferred_element_type=jnp.float32)
    to_tower = jnp.dot(near_tower.reshape(count * CLUSTER, BINS * D), tower_weight, preferred_element_type=jnp.float32)
    return (plate_at, tower_at, to_plate.reshape(count, CLUSTER, D), to_tower.reshape(count, CLUSTER, D))

def reference(features, pair_index, bins, plate_weight, tower_weight, norm_gain, update_in, update_out):
    grid = features.reshape(N_ROW, N_COL, HOME_DEV, CLUSTER, D)
    group = 8

    def device_step(total, device):
        row_at = device // N_COL
        col_at = device % N_COL
        plate = lax.dynamic_index_in_dim(grid, row_at, 0, keepdims=False).reshape(N_COL * HOME_DEV, CLUSTER, D)
        tower = lax.dynamic_index_in_dim(grid, col_at, 1, keepdims=False).reshape(N_ROW * HOME_DEV, CLUSTER, D)

        def block_step(inner, turn):
            plate_part, tower_part = inner
            start = (device * PAIRS_DEV + turn * group).astype(jnp.int32)
            plate_idx = lax.dynamic_slice_in_dim(pair_index[0], start, group)
            tower_idx = lax.dynamic_slice_in_dim(pair_index[1], start, group)
            block = lax.dynamic_slice_in_dim(bins, start, group, 0)
            plate_at, tower_at, to_plate, to_tower = pair_messages(plate, tower, plate_idx, tower_idx, block, plate_weight, tower_weight)
            plate_part = plate_part.at[plate_at].add(to_plate)
            tower_part = tower_part.at[tower_at].add(to_tower)
            return ((plate_part, tower_part), None)
        start_parts = (jnp.zeros((N_COL * HOME_DEV, CLUSTER, D), jnp.float32), jnp.zeros((N_ROW * HOME_DEV, CLUSTER, D), jnp.float32))
        (plate_part, tower_part), _ = lax.scan(block_step, start_parts, jnp.arange(PAIRS_DEV // group, dtype=jnp.int32))
        plate_round = lax.optimization_barrier(plate_part.astype(jnp.bfloat16)).astype(jnp.float32)
        tower_round = lax.optimization_barrier(tower_part.astype(jnp.bfloat16)).astype(jnp.float32)
        total = total.at[row_at].add(plate_round.reshape(N_COL, HOME_DEV, CLUSTER, D))
        total = total.at[:, col_at].add(tower_round.reshape(N_ROW, HOME_DEV, CLUSTER, D))
        return (total, None)
    start_total = jnp.zeros((N_ROW, N_COL, HOME_DEV, CLUSTER, D), jnp.float32)
    total, _ = lax.scan(device_step, start_total, jnp.arange(N_ROW * N_COL, dtype=jnp.int32))
    incoming = total.reshape(CLUSTERS * CLUSTER, D)
    scale = lax.rsqrt(lax.optimization_barrier(jnp.mean(incoming * incoming, axis=1, keepdims=True)) + 1e-06)
    normed = (incoming * scale * norm_gain[None, :]).astype(jnp.bfloat16)
    joined = jnp.concatenate([features, normed], axis=1)
    hidden = jax.nn.silu(jnp.dot(joined, update_in, preferred_element_type=jnp.float32)).astype(jnp.bfloat16)
    result = features.astype(jnp.float32) + jnp.dot(hidden, update_out, preferred_element_type=jnp.float32)
    return result.astype(jnp.bfloat16)
```

```python
import functools

import jax
import jax.numpy as jnp
from jax import lax
from jax.experimental import pallas as pl
from jax.experimental.pallas import tpu as pltpu
from jax.sharding import PartitionSpec as P

D = 128
CLUSTER = 128
BINS = 8
GROUP = 8


def side_kernel(transposed, own_row, idx_ref, far_ref, weight_ref, bins_ref, out_ref, table, acc):
    step = pl.program_id(0)

    @pl.when(step == 0)
    def _():
        acc[...] = jnp.zeros_like(acc)

        @pl.loop(0, table.shape[0])
        def _(c):
            rows = far_ref[pl.ds(pl.multiple_of(c * CLUSTER, CLUSTER), CLUSTER), :]
            mapped = jnp.dot(rows, weight_ref[...], preferred_element_type=jnp.float32)
            for k in range(BINS):
                table[c, k * CLUSTER:(k + 1) * CLUSTER, :] = mapped[:, k * D:(k + 1) * D].astype(jnp.bfloat16)

    @pl.when(idx_ref[0, step * GROUP] >= 0)
    def _():
        for g in range(GROUP):
            own = idx_ref[own_row, step * GROUP + g]
            far = idx_ref[1 - own_row, step * GROUP + g]
            live = own >= 0
            block = jnp.where(live, bins_ref[g], BINS).astype(jnp.float32)
            if transposed:
                block = block.T
            block = block.astype(jnp.bfloat16)
            one = jnp.ones_like(block)
            zero = jnp.zeros_like(block)
            basis = jnp.concatenate(
                [jnp.where(block == jnp.bfloat16(k), one, zero) for k in range(BINS)], axis=1
            )
            own = jnp.maximum(own, 0)
            far = jnp.maximum(far, 0)
            acc[own] += jnp.dot(basis, table[far], preferred_element_type=jnp.float32)

    @pl.when(step == pl.num_programs(0) - 1)
    def _():
        out_ref[...] = acc[...].astype(jnp.bfloat16)


def side(pair_index, far, weight, bins, own_clusters, own_row):
    slots = bins.shape[0]
    far_clusters = far.shape[0] // CLUSTER
    whole = lambda *_: (0, 0)
    wide = weight.reshape(BINS, D, D).transpose(1, 0, 2).reshape(D, BINS * D)
    return pl.pallas_call(
        functools.partial(side_kernel, own_row == 1, own_row),
        grid_spec=pltpu.PrefetchScalarGridSpec(
            num_scalar_prefetch=1,
            grid=(slots // GROUP,),
            in_specs=[
                pl.BlockSpec(far.shape, whole, pipeline_mode=pl.Buffered(1)),
                pl.BlockSpec(wide.shape, whole, pipeline_mode=pl.Buffered(1)),
                pl.BlockSpec((GROUP, CLUSTER, CLUSTER), lambda s, _: (s, 0, 0)),
            ],
            out_specs=pl.BlockSpec(
                (own_clusters, CLUSTER, D), lambda *_: (0, 0, 0), pipeline_mode=pl.Buffered(1)
            ),
            scratch_shapes=[
                pltpu.VMEM((far_clusters, BINS * CLUSTER, D), jnp.bfloat16),
                pltpu.VMEM((own_clusters, CLUSTER, D), jnp.float32),
            ],
        ),
        out_shape=jax.ShapeDtypeStruct((own_clusters, CLUSTER, D), jnp.bfloat16),
        compiler_params=pltpu.CompilerParams(vmem_limit_bytes=60 * 1024 * 1024),
    )(pair_index, far, wide, bins)


def shards(
    features, pair_index, bins, plate_weight, tower_weight, norm_gain, update_in, update_out
):
    tower = lax.all_gather(features, "row", axis=0, tiled=True)
    plate = lax.all_gather(features, "col", axis=0, tiled=True)
    plates = plate.shape[0] // CLUSTER
    towers = tower.shape[0] // CLUSTER
    plate_part = side(pair_index, tower, plate_weight, bins, plates, 0)
    tower_part = side(pair_index, plate, tower_weight, bins, towers, 1)
    plate_back = lax.psum_scatter(plate_part.reshape(-1, D), "col", scatter_dimension=0, tiled=True)
    tower_back = lax.psum_scatter(tower_part.reshape(-1, D), "row", scatter_dimension=0, tiled=True)
    incoming = plate_back.astype(jnp.float32) + tower_back.astype(jnp.float32)
    scale = lax.rsqrt(jnp.mean(incoming * incoming, axis=1, keepdims=True) + 1e-06)
    normed = (incoming * scale * norm_gain[None, :]).astype(jnp.bfloat16)
    joined = jnp.concatenate([features, normed], axis=1)
    hidden = jax.nn.silu(jnp.dot(joined, update_in, preferred_element_type=jnp.float32)).astype(
        jnp.bfloat16
    )
    result = features.astype(jnp.float32) + jnp.dot(
        hidden, update_out, preferred_element_type=jnp.float32
    )
    return result.astype(jnp.bfloat16)


def solution(mesh):
    placed = (
        P(("row", "col"), None),
        P(None, ("row", "col")),
        P(("row", "col"), None, None),
        P(),
        P(),
        P(),
        P(),
        P(),
    )
    return jax.shard_map(
        shards, mesh=mesh, in_specs=placed, out_specs=P(("row", "col"), None), check_vma=False
    )
```

```python
import functools

import jax
import jax.numpy as jnp
from jax import lax
from jax.experimental import pallas as pl
from jax.experimental.pallas import tpu as pltpu
from jax.sharding import PartitionSpec as P

D = 128
CLUSTER = 128
BINS = 8
GROUP = 8
CORES = 2


def side_kernel(own_row, n_far, n_own, idx_ref, far_at_ref, own_at_ref, *refs):
    far_refs = refs[:n_far]
    weight_ref, bins_ref = refs[n_far:n_far + 2]
    out_refs = refs[n_far + 2:n_far + 2 + n_own]
    wide, table, acc = refs[n_far + 2 + n_own:]
    step = pl.program_id(0)

    @pl.when(step == 0)
    def _():
        acc[...] = jnp.zeros_like(acc)
        for k in range(BINS):
            wide[:, k * D:(k + 1) * D] = weight_ref[k * D:(k + 1) * D, :]
        for n, far_ref in enumerate(far_refs):
            held = far_ref.shape[0] // CLUSTER
            first = far_at_ref[n] * held

            @pl.loop(0, held)
            def _(c):
                rows = far_ref[pl.ds(pl.multiple_of(c * CLUSTER, CLUSTER), CLUSTER), :]
                mapped = jnp.dot(rows, wide[...], preferred_element_type=jnp.float32)
                for k in range(BINS):
                    table[first + c, k * CLUSTER:(k + 1) * CLUSTER, :] = mapped[
                        :, k * D:(k + 1) * D
                    ].astype(jnp.bfloat16)

    @pl.when(idx_ref[0, step * GROUP] >= 0)
    def _():
        for g in range(GROUP):
            own = idx_ref[own_row, step * GROUP + g]
            far = idx_ref[1 - own_row, step * GROUP + g]
            live = own >= 0
            block = jnp.where(live, bins_ref[g], BINS).astype(jnp.float32)
            if own_row == 1:
                block = block.T
            block = block.astype(jnp.bfloat16)
            one = jnp.ones_like(block)
            zero = jnp.zeros_like(block)
            basis = jnp.concatenate(
                [jnp.where(block == jnp.bfloat16(k), one, zero) for k in range(BINS)], axis=1
            )
            own = jnp.maximum(own, 0)
            far = jnp.maximum(far, 0)
            acc[own] += jnp.dot(basis, table[far], preferred_element_type=jnp.float32)

    @pl.when(step == pl.num_programs(0) - 1)
    def _():
        for n, out_ref in enumerate(out_refs):
            held = out_ref.shape[0] // CLUSTER
            first = own_at_ref[n] * held

            @pl.loop(0, held)
            def _(c):
                rows = pl.ds(pl.multiple_of(c * CLUSTER, CLUSTER), CLUSTER)
                out_ref[rows, :] = acc[first + c].astype(jnp.bfloat16)


def side(pair_index, far, far_at, own_at, weight, bins, own_row):
    slots = bins.shape[0]
    rows = far[0].shape[0]
    held = rows // CLUSTER
    n_far, n_own = len(far), len(own_at)
    whole = lambda *_: (0, 0)
    once = pl.Buffered(1)
    scratch = (n_far * BINS + 2 * n_own + 2 * n_far + 2 * n_own) * rows * D * 2
    limit = max(scratch + 6 * 2**20, 54 * 2**20)
    flops = 2 * slots * CLUSTER * BINS * CLUSTER * D + 2 * n_far * rows * D * BINS * D
    return pl.pallas_call(
        functools.partial(side_kernel, own_row, n_far, n_own),
        grid_spec=pltpu.PrefetchScalarGridSpec(
            num_scalar_prefetch=3,
            grid=(slots // GROUP,),
            in_specs=[pl.BlockSpec((rows, D), whole, pipeline_mode=once)] * n_far
            + [
                pl.BlockSpec(weight.shape, whole, pipeline_mode=once),
                pl.BlockSpec((GROUP, CLUSTER, CLUSTER), lambda s, *_: (s, 0, 0)),
            ],
            out_specs=[pl.BlockSpec((rows, D), whole, pipeline_mode=once)] * n_own,
            scratch_shapes=[
                pltpu.VMEM((D, BINS * D), jnp.bfloat16),
                pltpu.VMEM((n_far * held, BINS * CLUSTER, D), jnp.bfloat16),
                pltpu.VMEM((n_own * held, CLUSTER, D), jnp.float32),
            ],
        ),
        out_shape=[jax.ShapeDtypeStruct((rows, D), jnp.bfloat16)] * n_own,
        compiler_params=pltpu.CompilerParams(vmem_limit_bytes=limit),
        cost_estimate=pl.CostEstimate(
            flops=3 * flops, bytes_accessed=4 * bins.size, transcendentals=0
        ),
    )(pair_index, jnp.stack(far_at), jnp.stack(own_at), *far, weight, bins)


def update_kernel(n_parts, features_ref, gain_ref, in_ref, out_w_ref, *refs):
    parts, out_ref = refs[:n_parts], refs[n_parts]
    incoming = parts[0][...].astype(jnp.float32)
    for part in parts[1:]:
        incoming = incoming + part[...].astype(jnp.float32)
    scale = lax.rsqrt(jnp.mean(incoming * incoming, axis=1, keepdims=True) + 1e-06)
    normed = (incoming * scale * gain_ref[...]).astype(jnp.bfloat16)
    features = features_ref[...]
    joined = jnp.concatenate([features, normed], axis=1)
    value = jnp.dot(joined, in_ref[...], preferred_element_type=jnp.float32)
    hidden = (value / (1.0 + jnp.exp(-value))).astype(jnp.bfloat16)
    out_ref[...] = (
        features.astype(jnp.float32)
        + jnp.dot(hidden, out_w_ref[...], preferred_element_type=jnp.float32)
    ).astype(jnp.bfloat16)


def update(features, gain, update_in, update_out, parts):
    rows = features.shape[0]
    tile = rows // 4
    block = pl.BlockSpec((tile, D), lambda t: (t, 0))
    whole = lambda *_: (0, 0)
    return pl.pallas_call(
        functools.partial(update_kernel, len(parts)),
        grid=(rows // tile,),
        in_specs=[
            block,
            pl.BlockSpec((1, D), whole),
            pl.BlockSpec(update_in.shape, whole),
            pl.BlockSpec(update_out.shape, whole),
        ]
        + [block] * len(parts),
        out_specs=block,
        out_shape=jax.ShapeDtypeStruct((rows, D), jnp.bfloat16),
        compiler_params=pltpu.CompilerParams(vmem_limit_bytes=16 * 2**20),
    )(features, gain.reshape(1, D), update_in, update_out, *parts)


def shards(
    n_row, n_col,
    features, pair_index, bins, plate_weight, tower_weight, norm_gain, update_in, update_out
):
    row, col = lax.axis_index("row"), lax.axis_index("col")
    chips = n_col // CORES

    def over_row(x, s):
        return lax.ppermute(x, "row", [(i, i ^ s) for i in range(n_row)])

    def over_col(x, s):
        return lax.ppermute(x, "col", [(i, i ^ s) for i in range(n_col)])

    row_at = [row ^ s for s in range(n_row)]
    tower = [features] + [over_row(features, s) for s in range(1, n_row)]
    col_at = [col ^ s for s in range(n_col)]
    plate = [None] * n_col
    plate[0] = features
    plate[1] = over_col(features, 1)
    for s in range(1, chips):
        plate[CORES * s] = over_col(features, CORES * s)

    plate_part = side(pair_index, tower, row_at, col_at, plate_weight, bins, 0)
    met = [over_col(plate_part[CORES * s + 1], 1) for s in range(chips)]
    far_cores = [plate[CORES * s] for s in range(1, chips)]
    *far_cores, _ = lax.optimization_barrier((*far_cores, plate_part[0]))
    for s in range(1, chips):
        plate[CORES * s] = far_cores[s - 1]
        plate[CORES * s + 1] = over_col(far_cores[s - 1], 1)
    joint = [
        (plate_part[CORES * s].astype(jnp.float32) + met[s].astype(jnp.float32)).astype(jnp.bfloat16)
        for s in range(1, chips)
    ]
    *joint, pair_index = lax.optimization_barrier((*joint, pair_index))
    plate_back = [plate_part[0], met[0]] + [over_col(joint[s - 1], CORES * s) for s in range(1, chips)]

    tower_part = side(pair_index, plate, col_at, row_at, tower_weight, bins, 1)
    tower_back = [tower_part[0]] + [over_row(tower_part[s], s) for s in range(1, n_row)]
    return update(features, norm_gain, update_in, update_out, plate_back + tower_back)


def solution(mesh):
    placed = (
        P(("row", "col"), None),
        P(None, ("row", "col")),
        P(("row", "col"), None, None),
        P(),
        P(),
        P(),
        P(),
        P(),
    )
    body = functools.partial(shards, mesh.shape["row"], mesh.shape["col"])
    return jax.shard_map(
        body, mesh=mesh, in_specs=placed, out_specs=P(("row", "col"), None), check_vma=False
    )
```

```python
import functools

import jax
import jax.numpy as jnp
from jax import lax
from jax.experimental import pallas as pl
from jax.experimental.pallas import tpu as pltpu
from jax.sharding import PartitionSpec as P

D = 128
CLUSTER = 128
BINS = 8
GROUP = 16
CORES = 2
PAIR = 2


def side_kernel(own_row, n_far, n_own, idx_ref, far_at_ref, own_at_ref, *refs):
    far_refs = refs[:n_far]
    weight_ref, bins_ref = refs[n_far:n_far + 2]
    out_refs = refs[n_far + 2:n_far + 2 + n_own]
    wide, table, acc = refs[n_far + 2 + n_own:]
    step = pl.program_id(0)

    @pl.when(step == 0)
    def _():
        acc[...] = jnp.zeros_like(acc)
        for k in range(BINS):
            lanes = slice((k % PAIR) * D, (k % PAIR + 1) * D)
            wide[k // PAIR, :, lanes] = weight_ref[k * D:(k + 1) * D, :]
        for n, far_ref in enumerate(far_refs):
            held = far_ref.shape[0] // CLUSTER
            first = far_at_ref[n] * held

            @pl.loop(0, BINS // PAIR)
            def _(q):
                mapped = jnp.dot(far_ref[...], wide[q], preferred_element_type=jnp.float32)
                mapped = mapped.astype(jnp.bfloat16)
                for h in range(PAIR):
                    rows = pl.ds(pl.multiple_of((q * PAIR + h) * CLUSTER, CLUSTER), CLUSTER)
                    for c in range(held):
                        table[first + c, rows, :] = mapped[
                            c * CLUSTER:(c + 1) * CLUSTER, h * D:(h + 1) * D
                        ]

    @pl.when(idx_ref[0, step * GROUP] >= 0)
    def _():
        for g in range(GROUP):
            own = idx_ref[own_row, step * GROUP + g]
            far = idx_ref[1 - own_row, step * GROUP + g]
            live = own >= 0
            block = jnp.where(live, bins_ref[g], BINS).astype(jnp.float32)
            if own_row == 1:
                block = block.T
            block = block.astype(jnp.bfloat16)
            one = jnp.ones_like(block)
            zero = jnp.zeros_like(block)
            basis = jnp.concatenate(
                [jnp.where(block == jnp.bfloat16(k), one, zero) for k in range(BINS)], axis=1
            )
            own = jnp.maximum(own, 0)
            far = jnp.maximum(far, 0)
            acc[own] += jnp.dot(basis, table[far], preferred_element_type=jnp.float32)

    @pl.when(step == pl.num_programs(0) - 1)
    def _():
        for n, out_ref in enumerate(out_refs):
            held = out_ref.shape[0] // CLUSTER
            first = own_at_ref[n] * held

            @pl.loop(0, held)
            def _(c):
                rows = pl.ds(pl.multiple_of(c * CLUSTER, CLUSTER), CLUSTER)
                out_ref[rows, :] = acc[first + c].astype(jnp.bfloat16)


def side(pair_index, far, far_at, own_at, weight, bins, own_row):
    slots = bins.shape[0]
    rows = far[0].shape[0]
    held = rows // CLUSTER
    n_far, n_own = len(far), len(own_at)
    whole = lambda *_: (0, 0)
    once = pl.Buffered(1)
    scratch = (n_far * BINS + 2 * n_own + 2 * n_far + 2 * n_own) * rows * D * 2
    limit = max(scratch + 6 * 2**20, 54 * 2**20)
    flops = 2 * slots * CLUSTER * BINS * CLUSTER * D + 2 * n_far * rows * D * BINS * D
    return pl.pallas_call(
        functools.partial(side_kernel, own_row, n_far, n_own),
        grid_spec=pltpu.PrefetchScalarGridSpec(
            num_scalar_prefetch=3,
            grid=(slots // GROUP,),
            in_specs=[pl.BlockSpec((rows, D), whole, pipeline_mode=once)] * n_far
            + [
                pl.BlockSpec(weight.shape, whole, pipeline_mode=once),
                pl.BlockSpec((GROUP, CLUSTER, CLUSTER), lambda s, *_: (s, 0, 0)),
            ],
            out_specs=[pl.BlockSpec((rows, D), whole, pipeline_mode=once)] * n_own,
            scratch_shapes=[
                pltpu.VMEM((BINS // PAIR, D, PAIR * D), jnp.bfloat16),
                pltpu.VMEM((n_far * held, BINS * CLUSTER, D), jnp.bfloat16),
                pltpu.VMEM((n_own * held, CLUSTER, D), jnp.float32),
            ],
        ),
        out_shape=[jax.ShapeDtypeStruct((rows, D), jnp.bfloat16)] * n_own,
        compiler_params=pltpu.CompilerParams(vmem_limit_bytes=limit),
        cost_estimate=pl.CostEstimate(
            flops=3 * flops, bytes_accessed=4 * bins.size, transcendentals=0
        ),
    )(pair_index, jnp.stack(far_at), jnp.stack(own_at), *far, weight, bins)


def update_kernel(n_parts, features_ref, gain_ref, in_ref, out_w_ref, *refs):
    parts, out_ref = refs[:n_parts], refs[n_parts]
    incoming = parts[0][...].astype(jnp.float32)
    for part in parts[1:]:
        incoming = incoming + part[...].astype(jnp.float32)
    scale = lax.rsqrt(jnp.mean(incoming * incoming, axis=1, keepdims=True) + 1e-06)
    normed = (incoming * scale * gain_ref[...]).astype(jnp.bfloat16)
    features = features_ref[...]
    joined = jnp.concatenate([features, normed], axis=1)
    value = jnp.dot(joined, in_ref[...], preferred_element_type=jnp.float32)
    hidden = (value / (1.0 + jnp.exp(-value))).astype(jnp.bfloat16)
    out_ref[...] = (
        features.astype(jnp.float32)
        + jnp.dot(hidden, out_w_ref[...], preferred_element_type=jnp.float32)
    ).astype(jnp.bfloat16)


def update(features, gain, update_in, update_out, parts):
    rows = features.shape[0]
    tile = rows // 4
    block = pl.BlockSpec((tile, D), lambda t: (t, 0))
    whole = lambda *_: (0, 0)
    return pl.pallas_call(
        functools.partial(update_kernel, len(parts)),
        grid=(rows // tile,),
        in_specs=[
            block,
            pl.BlockSpec((1, D), whole),
            pl.BlockSpec(update_in.shape, whole),
            pl.BlockSpec(update_out.shape, whole),
        ]
        + [block] * len(parts),
        out_specs=block,
        out_shape=jax.ShapeDtypeStruct((rows, D), jnp.bfloat16),
        compiler_params=pltpu.CompilerParams(vmem_limit_bytes=16 * 2**20),
    )(features, gain.reshape(1, D), update_in, update_out, *parts)


def shards(
    n_row, n_col,
    features, pair_index, bins, plate_weight, tower_weight, norm_gain, update_in, update_out
):
    row, col = lax.axis_index("row"), lax.axis_index("col")
    chips = n_col // CORES

    def over_row(x, s):
        return lax.ppermute(x, "row", [(i, i ^ s) for i in range(n_row)])

    def over_col(x, s):
        return lax.ppermute(x, "col", [(i, i ^ s) for i in range(n_col)])

    row_at = [row ^ s for s in range(n_row)]
    tower = [features] + [over_row(features, s) for s in range(1, n_row)]
    col_at = [col ^ s for s in range(n_col)]
    plate = [None] * n_col
    plate[0] = features
    plate[1] = over_col(features, 1)
    for s in range(1, chips):
        plate[CORES * s] = over_col(features, CORES * s)

    plate_part = side(pair_index, tower, row_at, col_at, plate_weight, bins, 0)
    met = [over_col(plate_part[CORES * s + 1], 1) for s in range(chips)]
    far_cores = [plate[CORES * s] for s in range(1, chips)]
    *far_cores, _ = lax.optimization_barrier((*far_cores, plate_part[0]))
    for s in range(1, chips):
        plate[CORES * s] = far_cores[s - 1]
        plate[CORES * s + 1] = over_col(far_cores[s - 1], 1)
    joint = [
        (plate_part[CORES * s].astype(jnp.float32) + met[s].astype(jnp.float32)).astype(jnp.bfloat16)
        for s in range(1, chips)
    ]
    *joint, pair_index = lax.optimization_barrier((*joint, pair_index))
    plate_back = [plate_part[0], met[0]] + [over_col(joint[s - 1], CORES * s) for s in range(1, chips)]

    tower_part = side(pair_index, plate, col_at, row_at, tower_weight, bins, 1)
    tower_back = [tower_part[0]] + [over_row(tower_part[s], s) for s in range(1, n_row)]
    return update(features, norm_gain, update_in, update_out, plate_back + tower_back)


def solution(mesh):
    placed = (
        P(("row", "col"), None),
        P(None, ("row", "col")),
        P(("row", "col"), None, None),
        P(),
        P(),
        P(),
        P(),
        P(),
    )
    body = functools.partial(shards, mesh.shape["row"], mesh.shape["col"])
    return jax.shard_map(
        body, mesh=mesh, in_specs=placed, out_specs=P(("row", "col"), None), check_vma=False
    )
```

```python
import functools

import jax
import jax.numpy as jnp
from jax import lax
from jax.experimental import pallas as pl
from jax.experimental.pallas import tpu as pltpu
from jax.sharding import PartitionSpec as P

D = 128
CLUSTER = 128
BINS = 8
GROUP = 16
CORES = 2
PAIR = 2
DEPTH = 4


def side_kernel(own_row, n_far, n_own, idx_ref, far_at_ref, own_at_ref, *refs):
    far_hbm, refs = refs[:n_far], refs[n_far:]
    weight_hbm, bins_hbm, refs = refs[0], refs[1], refs[2:]
    out_hbm, refs = refs[:n_own], refs[n_own:]
    far, weight, blocks, stage, wide, table, acc, far_sem, weight_sem, bins_sem, out_sem = refs
    held = far.shape[1] // CLUSTER
    steps = bins_hbm.shape[0] // GROUP

    def fetch(step, slot):
        at = pl.ds(pl.multiple_of(step * GROUP, GROUP), GROUP)
        return pltpu.make_async_copy(bins_hbm.at[at], blocks.at[slot], bins_sem.at[slot])

    weight_copy = pltpu.make_async_copy(weight_hbm, weight, weight_sem)
    weight_copy.start()
    far_copies = [
        pltpu.make_async_copy(far_hbm[n], far.at[n], far_sem.at[n]) for n in range(n_far)
    ]
    for copy in far_copies:
        copy.start()
    for step in range(DEPTH):
        fetch(step, step).start()

    acc[...] = jnp.zeros_like(acc)
    weight_copy.wait()
    for k in range(BINS):
        lanes = slice((k % PAIR) * D, (k % PAIR + 1) * D)
        wide[k // PAIR, :, lanes] = weight[k * D:(k + 1) * D, :]
    for n in range(n_far):
        first = far_at_ref[n] * held
        far_copies[n].wait()

        @pl.loop(0, BINS // PAIR)
        def _(q):
            mapped = jnp.dot(far[n], wide[q], preferred_element_type=jnp.float32)
            mapped = mapped.astype(jnp.bfloat16)
            for h in range(PAIR):
                rows = pl.ds(pl.multiple_of((q * PAIR + h) * CLUSTER, CLUSTER), CLUSTER)
                for c in range(held):
                    table[first + c, rows, :] = mapped[
                        c * CLUSTER:(c + 1) * CLUSTER, h * D:(h + 1) * D
                    ]

    @pl.loop(0, steps)
    def _(step):
        slot = lax.rem(step, DEPTH)
        fetch(step, slot).wait()

        @pl.when(idx_ref[0, step * GROUP] >= 0)
        def _():
            for g in range(GROUP):
                own = idx_ref[own_row, step * GROUP + g]
                other = idx_ref[1 - own_row, step * GROUP + g]
                live = own >= 0
                block = jnp.where(live, blocks[slot, g], BINS).astype(jnp.float32)
                if own_row == 1:
                    block = block.T
                block = block.astype(jnp.bfloat16)
                one = jnp.ones_like(block)
                zero = jnp.zeros_like(block)
                basis = jnp.concatenate(
                    [jnp.where(block == jnp.bfloat16(k), one, zero) for k in range(BINS)], axis=1
                )
                own = jnp.maximum(own, 0)
                other = jnp.maximum(other, 0)
                acc[own] += jnp.dot(basis, table[other], preferred_element_type=jnp.float32)

        @pl.when(step + DEPTH < steps)
        def _():
            fetch(step + DEPTH, slot).start()

    out_copies = []
    for n in range(n_own):
        first = own_at_ref[n] * held
        for c in range(held):
            stage[n, c * CLUSTER:(c + 1) * CLUSTER, :] = acc[first + c].astype(jnp.bfloat16)
        copy = pltpu.make_async_copy(stage.at[n], out_hbm[n], out_sem.at[n])
        copy.start()
        out_copies.append(copy)
    for copy in out_copies:
        copy.wait()


def side(pair_index, far, far_at, own_at, weight, bins, own_row):
    slots = bins.shape[0]
    rows = far[0].shape[0]
    held = rows // CLUSTER
    n_far, n_own = len(far), len(own_at)
    scratch = (n_far * (BINS + 1) + 3 * n_own) * rows * D * 2 + DEPTH * GROUP * CLUSTER * CLUSTER * 4
    limit = max(scratch + 6 * 2**20, 54 * 2**20)
    flops = 2 * slots * CLUSTER * BINS * CLUSTER * D + 2 * n_far * rows * D * BINS * D
    scalar = pl.BlockSpec(memory_space=pltpu.SMEM)
    placed = pl.BlockSpec(memory_space=pl.ANY)
    return pl.pallas_call(
        functools.partial(side_kernel, own_row, n_far, n_own),
        in_specs=[scalar] * 3 + [placed] * (n_far + 2),
        out_specs=[placed] * n_own,
        scratch_shapes=[
            pltpu.VMEM((n_far, rows, D), jnp.bfloat16),
            pltpu.VMEM(weight.shape, jnp.bfloat16),
            pltpu.VMEM((DEPTH, GROUP, CLUSTER, CLUSTER), jnp.int32),
            pltpu.VMEM((n_own, rows, D), jnp.bfloat16),
            pltpu.VMEM((BINS // PAIR, D, PAIR * D), jnp.bfloat16),
            pltpu.VMEM((n_far * held, BINS * CLUSTER, D), jnp.bfloat16),
            pltpu.VMEM((n_own * held, CLUSTER, D), jnp.float32),
            pltpu.SemaphoreType.DMA((n_far,)),
            pltpu.SemaphoreType.DMA,
            pltpu.SemaphoreType.DMA((DEPTH,)),
            pltpu.SemaphoreType.DMA((n_own,)),
        ],
        out_shape=[jax.ShapeDtypeStruct((rows, D), jnp.bfloat16)] * n_own,
        compiler_params=pltpu.CompilerParams(vmem_limit_bytes=limit),
        cost_estimate=pl.CostEstimate(
            flops=3 * flops, bytes_accessed=4 * bins.size, transcendentals=0
        ),
    )(pair_index, jnp.stack(far_at), jnp.stack(own_at), *far, weight, bins)


def update_kernel(n_parts, features_ref, gain_ref, in_ref, out_w_ref, *refs):
    parts, out_ref = refs[:n_parts], refs[n_parts]
    incoming = parts[0][...].astype(jnp.float32)
    for part in parts[1:]:
        incoming = incoming + part[...].astype(jnp.float32)
    scale = lax.rsqrt(jnp.mean(incoming * incoming, axis=1, keepdims=True) + 1e-06)
    normed = (incoming * scale * gain_ref[...]).astype(jnp.bfloat16)
    features = features_ref[...]
    joined = jnp.concatenate([features, normed], axis=1)
    value = jnp.dot(joined, in_ref[...], preferred_element_type=jnp.float32)
    hidden = (value / (1.0 + jnp.exp(-value))).astype(jnp.bfloat16)
    out_ref[...] = (
        features.astype(jnp.float32)
        + jnp.dot(hidden, out_w_ref[...], preferred_element_type=jnp.float32)
    ).astype(jnp.bfloat16)


def update(features, gain, update_in, update_out, parts):
    rows = features.shape[0]
    tile = rows // 4
    block = pl.BlockSpec((tile, D), lambda t: (t, 0))
    whole = lambda *_: (0, 0)
    return pl.pallas_call(
        functools.partial(update_kernel, len(parts)),
        grid=(rows // tile,),
        in_specs=[
            block,
            pl.BlockSpec((1, D), whole),
            pl.BlockSpec(update_in.shape, whole),
            pl.BlockSpec(update_out.shape, whole),
        ]
        + [block] * len(parts),
        out_specs=block,
        out_shape=jax.ShapeDtypeStruct((rows, D), jnp.bfloat16),
        compiler_params=pltpu.CompilerParams(vmem_limit_bytes=16 * 2**20),
    )(features, gain.reshape(1, D), update_in, update_out, *parts)


def shards(
    n_row, n_col,
    features, pair_index, bins, plate_weight, tower_weight, norm_gain, update_in, update_out
):
    row, col = lax.axis_index("row"), lax.axis_index("col")
    chips = n_col // CORES

    def over_row(x, s):
        return lax.ppermute(x, "row", [(i, i ^ s) for i in range(n_row)])

    def over_col(x, s):
        return lax.ppermute(x, "col", [(i, i ^ s) for i in range(n_col)])

    row_at = [row ^ s for s in range(n_row)]
    tower = [features] + [over_row(features, s) for s in range(1, n_row)]
    col_at = [col ^ s for s in range(n_col)]
    plate = [None] * n_col
    plate[0] = features
    plate[1] = over_col(features, 1)
    for s in range(1, chips):
        plate[CORES * s] = over_col(features, CORES * s)

    plate_part = side(pair_index, tower, row_at, col_at, plate_weight, bins, 0)
    met = [over_col(plate_part[CORES * s + 1], 1) for s in range(chips)]
    far_cores = [plate[CORES * s] for s in range(1, chips)]
    *far_cores, _ = lax.optimization_barrier((*far_cores, plate_part[0]))
    for s in range(1, chips):
        plate[CORES * s] = far_cores[s - 1]
        plate[CORES * s + 1] = over_col(far_cores[s - 1], 1)
    joint = [
        (plate_part[CORES * s].astype(jnp.float32) + met[s].astype(jnp.float32)).astype(jnp.bfloat16)
        for s in range(1, chips)
    ]
    *joint, pair_index = lax.optimization_barrier((*joint, pair_index))
    plate_back = [plate_part[0], met[0]] + [over_col(joint[s - 1], CORES * s) for s in range(1, chips)]

    tower_part = side(pair_index, plate, col_at, row_at, tower_weight, bins, 1)
    tower_back = [tower_part[0]] + [over_row(tower_part[s], s) for s in range(1, n_row)]
    return update(features, norm_gain, update_in, update_out, plate_back + tower_back)


def solution(mesh):
    placed = (
        P(("row", "col"), None),
        P(None, ("row", "col")),
        P(("row", "col"), None, None),
        P(),
        P(),
        P(),
        P(),
        P(),
    )
    body = functools.partial(shards, mesh.shape["row"], mesh.shape["col"])
    return jax.shard_map(
        body, mesh=mesh, in_specs=placed, out_specs=P(("row", "col"), None), check_vma=False
    )
```

```python
import functools

import jax
import jax.numpy as jnp
from jax import lax
from jax.experimental import pallas as pl
from jax.experimental.pallas import tpu as pltpu
from jax.sharding import PartitionSpec as P

D = 128
CLUSTER = 128
BINS = 8
GROUP = 16
CORES = 2
PAIR = 2
DEPTH = 4


def fill(table, first, rows_of, wide):
    held = rows_of.shape[0] // CLUSTER

    @pl.loop(0, BINS // PAIR)
    def _(q):
        mapped = jnp.dot(rows_of[...], wide[q], preferred_element_type=jnp.float32)
        mapped = mapped.astype(jnp.bfloat16)
        for h in range(PAIR):
            rows = pl.ds(pl.multiple_of((q * PAIR + h) * CLUSTER, CLUSTER), CLUSTER)
            for c in range(held):
                table[first + c, rows, :] = mapped[
                    c * CLUSTER:(c + 1) * CLUSTER, h * D:(h + 1) * D
                ]


def widen(wide, weight):
    for k in range(BINS):
        lanes = slice((k % PAIR) * D, (k % PAIR + 1) * D)
        wide[k // PAIR, :, lanes] = weight[k * D:(k + 1) * D, :]


def ready_kernel(rows_ref, weight_ref, table_ref, wide):
    widen(wide, weight_ref)
    fill(table_ref, 0, rows_ref, wide)


def ready_table(block, weight):
    rows = block.shape[0]
    held = rows // CLUSTER
    shape = (held, BINS * CLUSTER, D)
    return pl.pallas_call(
        ready_kernel,
        in_specs=[pl.BlockSpec(memory_space=pltpu.VMEM)] * 2,
        out_specs=pl.BlockSpec(memory_space=pltpu.VMEM),
        out_shape=jax.ShapeDtypeStruct(shape, jnp.bfloat16),
        scratch_shapes=[pltpu.VMEM((BINS // PAIR, D, PAIR * D), jnp.bfloat16)],
        compiler_params=pltpu.CompilerParams(vmem_limit_bytes=12 * 2**20),
        cost_estimate=pl.CostEstimate(
            flops=6 * rows * D * BINS * D, bytes_accessed=2 * rows * D * BINS, transcendentals=0
        ),
    )(block, weight)


def side_kernel(own_row, n_far, n_own, ready, idx_ref, far_at_ref, own_at_ref, *refs):
    far_hbm, refs = refs[:n_far], refs[n_far:]
    weight_hbm, bins_hbm, refs = refs[0], refs[1], refs[2:]
    out_hbm, refs = refs[:n_own], refs[n_own:]
    far, weight, blocks, stage, wide, table, acc, far_sem, weight_sem, bins_sem, out_sem = refs
    held = far.shape[1] // CLUSTER
    steps = bins_hbm.shape[0] // GROUP

    def fetch(step, slot):
        at = pl.ds(pl.multiple_of(step * GROUP, GROUP), GROUP)
        return pltpu.make_async_copy(bins_hbm.at[at], blocks.at[slot], bins_sem.at[slot])

    weight_copy = pltpu.make_async_copy(weight_hbm, weight, weight_sem)
    weight_copy.start()
    far_copies = [
        pltpu.make_async_copy(
            far_hbm[n],
            table.at[pl.ds(far_at_ref[n] * held, held)] if n in ready else far.at[n],
            far_sem.at[n],
        )
        for n in range(n_far)
    ]
    for copy in far_copies:
        copy.start()
    for step in range(DEPTH):
        fetch(step, step).start()

    acc[...] = jnp.zeros_like(acc)
    weight_copy.wait()
    widen(wide, weight)
    for n in range(n_far):
        if n not in ready:
            far_copies[n].wait()
            fill(table, far_at_ref[n] * held, far.at[n], wide)
    for n in ready:
        far_copies[n].wait()

    @pl.loop(0, steps)
    def _(step):
        slot = lax.rem(step, DEPTH)
        fetch(step, slot).wait()

        @pl.when(idx_ref[0, step * GROUP] >= 0)
        def _():
            for g in range(GROUP):
                own = idx_ref[own_row, step * GROUP + g]
                other = idx_ref[1 - own_row, step * GROUP + g]
                live = own >= 0
                block = jnp.where(live, blocks[slot, g], BINS).astype(jnp.float32)
                if own_row == 1:
                    block = block.T
                block = block.astype(jnp.bfloat16)
                one = jnp.ones_like(block)
                zero = jnp.zeros_like(block)
                basis = jnp.concatenate(
                    [jnp.where(block == jnp.bfloat16(k), one, zero) for k in range(BINS)], axis=1
                )
                own = jnp.maximum(own, 0)
                other = jnp.maximum(other, 0)
                acc[own] += jnp.dot(basis, table[other], preferred_element_type=jnp.float32)

        @pl.when(step + DEPTH < steps)
        def _():
            fetch(step + DEPTH, slot).start()

    out_copies = []
    for n in range(n_own):
        first = own_at_ref[n] * held
        for c in range(held):
            stage[n, c * CLUSTER:(c + 1) * CLUSTER, :] = acc[first + c].astype(jnp.bfloat16)
        copy = pltpu.make_async_copy(stage.at[n], out_hbm[n], out_sem.at[n])
        copy.start()
        out_copies.append(copy)
    for copy in out_copies:
        copy.wait()


def side(pair_index, far, far_at, own_at, weight, bins, own_row, ready, rows):
    slots = bins.shape[0]
    held = rows // CLUSTER
    n_far, n_own = len(far), len(own_at)
    scratch = (n_far * (BINS + 1) + 3 * n_own) * rows * D * 2 + DEPTH * GROUP * CLUSTER * CLUSTER * 4
    limit = max(scratch + 6 * 2**20, 54 * 2**20)
    flops = 2 * slots * CLUSTER * BINS * CLUSTER * D + 2 * n_far * rows * D * BINS * D
    scalar = pl.BlockSpec(memory_space=pltpu.SMEM)
    placed = pl.BlockSpec(memory_space=pl.ANY)
    return pl.pallas_call(
        functools.partial(side_kernel, own_row, n_far, n_own, ready),
        in_specs=[scalar] * 3 + [placed] * (n_far + 2),
        out_specs=[placed] * n_own,
        scratch_shapes=[
            pltpu.VMEM((n_far, rows, D), jnp.bfloat16),
            pltpu.VMEM(weight.shape, jnp.bfloat16),
            pltpu.VMEM((DEPTH, GROUP, CLUSTER, CLUSTER), jnp.int32),
            pltpu.VMEM((n_own, rows, D), jnp.bfloat16),
            pltpu.VMEM((BINS // PAIR, D, PAIR * D), jnp.bfloat16),
            pltpu.VMEM((n_far * held, BINS * CLUSTER, D), jnp.bfloat16),
            pltpu.VMEM((n_own * held, CLUSTER, D), jnp.float32),
            pltpu.SemaphoreType.DMA((n_far,)),
            pltpu.SemaphoreType.DMA,
            pltpu.SemaphoreType.DMA((DEPTH,)),
            pltpu.SemaphoreType.DMA((n_own,)),
        ],
        out_shape=[jax.ShapeDtypeStruct((rows, D), jnp.bfloat16)] * n_own,
        compiler_params=pltpu.CompilerParams(vmem_limit_bytes=limit),
        cost_estimate=pl.CostEstimate(
            flops=3 * flops, bytes_accessed=4 * bins.size, transcendentals=0
        ),
    )(pair_index, jnp.stack(far_at), jnp.stack(own_at), *far, weight, bins)


def update_kernel(n_parts, features_ref, gain_ref, in_ref, out_w_ref, *refs):
    parts, out_ref = refs[:n_parts], refs[n_parts]
    incoming = parts[0][...].astype(jnp.float32)
    for part in parts[1:]:
        incoming = incoming + part[...].astype(jnp.float32)
    scale = lax.rsqrt(jnp.mean(incoming * incoming, axis=1, keepdims=True) + 1e-06)
    normed = (incoming * scale * gain_ref[...]).astype(jnp.bfloat16)
    features = features_ref[...]
    joined = jnp.concatenate([features, normed], axis=1)
    value = jnp.dot(joined, in_ref[...], preferred_element_type=jnp.float32)
    hidden = (value / (1.0 + jnp.exp(-value))).astype(jnp.bfloat16)
    out_ref[...] = (
        features.astype(jnp.float32)
        + jnp.dot(hidden, out_w_ref[...], preferred_element_type=jnp.float32)
    ).astype(jnp.bfloat16)


def update(features, gain, update_in, update_out, parts):
    rows = features.shape[0]
    tile = rows // 4
    block = pl.BlockSpec((tile, D), lambda t: (t, 0))
    whole = lambda *_: (0, 0)
    return pl.pallas_call(
        functools.partial(update_kernel, len(parts)),
        grid=(rows // tile,),
        in_specs=[
            block,
            pl.BlockSpec((1, D), whole),
            pl.BlockSpec(update_in.shape, whole),
            pl.BlockSpec(update_out.shape, whole),
        ]
        + [block] * len(parts),
        out_specs=block,
        out_shape=jax.ShapeDtypeStruct((rows, D), jnp.bfloat16),
        compiler_params=pltpu.CompilerParams(vmem_limit_bytes=16 * 2**20),
    )(features, gain.reshape(1, D), update_in, update_out, *parts)


def shards(
    n_row, n_col,
    features, pair_index, bins, plate_weight, tower_weight, norm_gain, update_in, update_out
):
    row, col = lax.axis_index("row"), lax.axis_index("col")
    chips = n_col // CORES

    def over_row(x, s):
        return lax.ppermute(x, "row", [(i, i ^ s) for i in range(n_row)])

    def over_col(x, s):
        return lax.ppermute(x, "col", [(i, i ^ s) for i in range(n_col)])

    row_at = [row ^ s for s in range(n_row)]
    tower = [features] + [over_row(features, s) for s in range(1, n_row)]
    col_at = [col ^ s for s in range(n_col)]
    plate = [None] * n_col
    plate[0] = features
    plate[1] = over_col(features, 1)
    for s in range(1, chips):
        plate[CORES * s] = over_col(features, CORES * s)

    rows = features.shape[0]
    tower[0] = ready_table(features, plate_weight)
    own_table = ready_table(features, tower_weight)
    plate_part = side(
        pair_index, tower, row_at, col_at, plate_weight, bins, 0, (0,), rows
    )
    met = [over_col(plate_part[CORES * s + 1], 1) for s in range(chips)]
    far_cores = [plate[CORES * s] for s in range(1, chips)]
    *far_cores, _ = lax.optimization_barrier((*far_cores, plate_part[0]))
    for s in range(1, chips):
        plate[CORES * s] = ready_table(far_cores[s - 1], tower_weight)
        plate[CORES * s + 1] = over_col(far_cores[s - 1], 1)
    joint = [
        (plate_part[CORES * s].astype(jnp.float32) + met[s].astype(jnp.float32)).astype(jnp.bfloat16)
        for s in range(1, chips)
    ]
    *joint, pair_index = lax.optimization_barrier((*joint, pair_index))
    plate_back = [plate_part[0], met[0]] + [over_col(joint[s - 1], CORES * s) for s in range(1, chips)]

    plate[0] = own_table
    ready = tuple(range(0, n_col, CORES))
    tower_part = side(
        pair_index, plate, col_at, row_at, tower_weight, bins, 1, ready, rows
    )
    tower_back = [tower_part[0]] + [over_row(tower_part[s], s) for s in range(1, n_row)]
    return update(features, norm_gain, update_in, update_out, plate_back + tower_back)


def solution(mesh):
    placed = (
        P(("row", "col"), None),
        P(None, ("row", "col")),
        P(("row", "col"), None, None),
        P(),
        P(),
        P(),
        P(),
        P(),
    )
    body = functools.partial(shards, mesh.shape["row"], mesh.shape["col"])
    return jax.shard_map(
        body, mesh=mesh, in_specs=placed, out_specs=P(("row", "col"), None), check_vma=False
    )
```

```python
import functools

import jax
import jax.numpy as jnp
from jax import lax
from jax.experimental import pallas as pl
from jax.experimental.pallas import tpu as pltpu
from jax.sharding import PartitionSpec as P

D = 128
CLUSTER = 128
BINS = 8
GROUP = 16
CORES = 2
PAIR = 2
DEPTH = 4


def fill(table, first, rows_of, wide):
    held = rows_of.shape[0] // CLUSTER

    @pl.loop(0, BINS // PAIR)
    def _(q):
        mapped = jnp.dot(rows_of[...], wide[q], preferred_element_type=jnp.float32)
        mapped = mapped.astype(jnp.bfloat16)
        for h in range(PAIR):
            rows = pl.ds(pl.multiple_of((q * PAIR + h) * CLUSTER, CLUSTER), CLUSTER)
            for c in range(held):
                table[first + c, rows, :] = mapped[
                    c * CLUSTER:(c + 1) * CLUSTER, h * D:(h + 1) * D
                ]


def widen(wide, weight):
    for k in range(BINS):
        lanes = slice((k % PAIR) * D, (k % PAIR + 1) * D)
        wide[k // PAIR, :, lanes] = weight[k * D:(k + 1) * D, :]


def ready_kernel(rows_ref, weight_ref, table_ref, wide):
    widen(wide, weight_ref)
    fill(table_ref, 0, rows_ref, wide)


def ready_table(block, weight):
    rows = block.shape[0]
    held = rows // CLUSTER
    shape = (held, BINS * CLUSTER, D)
    return pl.pallas_call(
        ready_kernel,
        in_specs=[pl.BlockSpec(memory_space=pltpu.VMEM)] * 2,
        out_specs=pl.BlockSpec(memory_space=pltpu.VMEM),
        out_shape=jax.ShapeDtypeStruct(shape, jnp.bfloat16),
        scratch_shapes=[pltpu.VMEM((BINS // PAIR, D, PAIR * D), jnp.bfloat16)],
        compiler_params=pltpu.CompilerParams(vmem_limit_bytes=12 * 2**20),
        cost_estimate=pl.CostEstimate(
            flops=6 * rows * D * BINS * D, bytes_accessed=2 * rows * D * BINS, transcendentals=0
        ),
    )(block, weight)


def side_kernel(own_row, n_far, n_own, ready, idx_ref, far_at_ref, own_at_ref, *refs):
    far_hbm, refs = refs[:n_far], refs[n_far:]
    weight_hbm, bins_hbm, refs = refs[0], refs[1], refs[2:]
    out_hbm, refs = refs[:n_own], refs[n_own:]
    far, weight, blocks, stage, wide, table, acc, far_sem, weight_sem, bins_sem, out_sem = refs
    held = far.shape[1] // CLUSTER
    steps = bins_hbm.shape[0] // GROUP

    def fetch(step, slot):
        at = pl.ds(pl.multiple_of(step * GROUP, GROUP), GROUP)
        return pltpu.make_async_copy(bins_hbm.at[at], blocks.at[slot], bins_sem.at[slot])

    weight_copy = pltpu.make_async_copy(weight_hbm, weight, weight_sem)
    weight_copy.start()
    far_copies = [
        pltpu.make_async_copy(
            far_hbm[n],
            table.at[pl.ds(far_at_ref[n] * held, held)] if n in ready else far.at[n],
            far_sem.at[n],
        )
        for n in range(n_far)
    ]
    for copy in far_copies:
        copy.start()
    for step in range(DEPTH):
        fetch(step, step).start()

    acc[...] = jnp.zeros_like(acc)
    weight_copy.wait()
    widen(wide, weight)
    for n in range(n_far):
        if n not in ready:
            far_copies[n].wait()
            fill(table, far_at_ref[n] * held, far.at[n], wide)
    for n in ready:
        far_copies[n].wait()

    @pl.loop(0, steps)
    def _(step):
        slot = lax.rem(step, DEPTH)
        fetch(step, slot).wait()

        @pl.when(idx_ref[0, step * GROUP] >= 0)
        def _():
            for g in range(GROUP):
                own = idx_ref[own_row, step * GROUP + g]
                other = idx_ref[1 - own_row, step * GROUP + g]
                live = own >= 0
                block = jnp.where(live, blocks[slot, g], BINS).astype(jnp.float32)
                if own_row == 1:
                    block = block.T
                block = block.astype(jnp.bfloat16)
                one = jnp.ones_like(block)
                zero = jnp.zeros_like(block)
                basis = jnp.concatenate(
                    [jnp.where(block == jnp.bfloat16(k), one, zero) for k in range(BINS)], axis=1
                )
                own = jnp.maximum(own, 0)
                other = jnp.maximum(other, 0)
                acc[own] += jnp.dot(basis, table[other], preferred_element_type=jnp.float32)

        @pl.when(step + DEPTH < steps)
        def _():
            fetch(step + DEPTH, slot).start()

    out_copies = []
    for n in range(n_own):
        first = own_at_ref[n] * held
        for c in range(held):
            stage[n, c * CLUSTER:(c + 1) * CLUSTER, :] = acc[first + c].astype(jnp.bfloat16)
        copy = pltpu.make_async_copy(stage.at[n], out_hbm[n], out_sem.at[n])
        copy.start()
        out_copies.append(copy)
    for copy in out_copies:
        copy.wait()


def side(pair_index, far, far_at, own_at, weight, bins, own_row, ready, rows):
    slots = bins.shape[0]
    held = rows // CLUSTER
    n_far, n_own = len(far), len(own_at)
    scratch = (n_far * (BINS + 1) + 3 * n_own) * rows * D * 2 + DEPTH * GROUP * CLUSTER * CLUSTER * 4
    limit = scratch + 3 * 2**20 if own_row == 1 else max(scratch + 3 * 2**20, 54 * 2**20)
    flops = 2 * slots * CLUSTER * BINS * CLUSTER * D + 2 * n_far * rows * D * BINS * D
    scalar = pl.BlockSpec(memory_space=pltpu.SMEM)
    placed = pl.BlockSpec(memory_space=pl.ANY)
    return pl.pallas_call(
        functools.partial(side_kernel, own_row, n_far, n_own, ready),
        in_specs=[scalar] * 3
        + [placed] * (n_far + 1)
        + [pl.BlockSpec(memory_space=pltpu.HBM)],
        out_specs=[placed] * n_own,
        scratch_shapes=[
            pltpu.VMEM((n_far, rows, D), jnp.bfloat16),
            pltpu.VMEM(weight.shape, jnp.bfloat16),
            pltpu.VMEM((DEPTH, GROUP, CLUSTER, CLUSTER), jnp.int32),
            pltpu.VMEM((n_own, rows, D), jnp.bfloat16),
            pltpu.VMEM((BINS // PAIR, D, PAIR * D), jnp.bfloat16),
            pltpu.VMEM((n_far * held, BINS * CLUSTER, D), jnp.bfloat16),
            pltpu.VMEM((n_own * held, CLUSTER, D), jnp.float32),
            pltpu.SemaphoreType.DMA((n_far,)),
            pltpu.SemaphoreType.DMA,
            pltpu.SemaphoreType.DMA((DEPTH,)),
            pltpu.SemaphoreType.DMA((n_own,)),
        ],
        out_shape=[jax.ShapeDtypeStruct((rows, D), jnp.bfloat16)] * n_own,
        compiler_params=pltpu.CompilerParams(vmem_limit_bytes=limit),
        cost_estimate=pl.CostEstimate(
            flops=3 * flops, bytes_accessed=4 * bins.size, transcendentals=0
        ),
    )(pair_index, jnp.stack(far_at), jnp.stack(own_at), *far, weight, bins)


def update_kernel(n_parts, features_ref, gain_ref, in_ref, out_w_ref, *refs):
    parts, out_ref = refs[:n_parts], refs[n_parts]
    incoming = parts[0][...].astype(jnp.float32)
    for part in parts[1:]:
        incoming = incoming + part[...].astype(jnp.float32)
    scale = lax.rsqrt(jnp.mean(incoming * incoming, axis=1, keepdims=True) + 1e-06)
    normed = (incoming * scale * gain_ref[...]).astype(jnp.bfloat16)
    features = features_ref[...]
    joined = jnp.concatenate([features, normed], axis=1)
    value = jnp.dot(joined, in_ref[...], preferred_element_type=jnp.float32)
    hidden = (value / (1.0 + jnp.exp(-value))).astype(jnp.bfloat16)
    out_ref[...] = (
        features.astype(jnp.float32)
        + jnp.dot(hidden, out_w_ref[...], preferred_element_type=jnp.float32)
    ).astype(jnp.bfloat16)


def update(features, gain, update_in, update_out, parts):
    rows = features.shape[0]
    tile = rows // 4
    block = pl.BlockSpec((tile, D), lambda t: (t, 0))
    whole = lambda *_: (0, 0)
    return pl.pallas_call(
        functools.partial(update_kernel, len(parts)),
        grid=(rows // tile,),
        in_specs=[
            block,
            pl.BlockSpec((1, D), whole),
            pl.BlockSpec(update_in.shape, whole),
            pl.BlockSpec(update_out.shape, whole),
        ]
        + [block] * len(parts),
        out_specs=block,
        out_shape=jax.ShapeDtypeStruct((rows, D), jnp.bfloat16),
        compiler_params=pltpu.CompilerParams(vmem_limit_bytes=16 * 2**20),
    )(features, gain.reshape(1, D), update_in, update_out, *parts)


def shards(
    n_row, n_col,
    features, pair_index, bins, plate_weight, tower_weight, norm_gain, update_in, update_out
):
    row, col = lax.axis_index("row"), lax.axis_index("col")
    chips = n_col // CORES

    def over_row(x, s):
        return lax.ppermute(x, "row", [(i, i ^ s) for i in range(n_row)])

    def over_col(x, s):
        return lax.ppermute(x, "col", [(i, i ^ s) for i in range(n_col)])

    row_at = [row ^ s for s in range(n_row)]
    tower = [features] + [over_row(features, s) for s in range(1, n_row)]
    col_at = [col ^ s for s in range(n_col)]
    plate = [None] * n_col
    plate[0] = features
    plate[1] = over_col(features, 1)
    for s in range(1, chips):
        plate[CORES * s] = over_col(features, CORES * s)

    rows = features.shape[0]
    tower[0] = ready_table(features, plate_weight)
    own_table = ready_table(features, tower_weight)
    plate_part = side(
        pair_index, tower, row_at, col_at, plate_weight, bins, 0, (0,), rows
    )
    met = [over_col(plate_part[CORES * s + 1], 1) for s in range(chips)]
    far_cores = [plate[CORES * s] for s in range(1, chips)]
    *far_cores, _ = lax.optimization_barrier((*far_cores, plate_part[0]))
    for s in range(1, chips):
        plate[CORES * s] = ready_table(far_cores[s - 1], tower_weight)
        plate[CORES * s + 1] = over_col(far_cores[s - 1], 1)
    joint = [
        (plate_part[CORES * s].astype(jnp.float32) + met[s].astype(jnp.float32)).astype(jnp.bfloat16)
        for s in range(1, chips)
    ]
    *joint, pair_index = lax.optimization_barrier((*joint, pair_index))
    plate_back = [plate_part[0], met[0]] + [over_col(joint[s - 1], CORES * s) for s in range(1, chips)]

    plate[0] = own_table
    ready = tuple(range(0, n_col, CORES))
    tower_part = side(
        pair_index, plate, col_at, row_at, tower_weight, bins, 1, ready, rows
    )
    tower_back = [tower_part[0]] + [over_row(tower_part[s], s) for s in range(1, n_row)]
    return update(features, norm_gain, update_in, update_out, plate_back + tower_back)


def solution(mesh):
    placed = (
        P(("row", "col"), None),
        P(None, ("row", "col")),
        P(("row", "col"), None, None),
        P(),
        P(),
        P(),
        P(),
        P(),
    )
    body = functools.partial(shards, mesh.shape["row"], mesh.shape["col"])
    return jax.shard_map(
        body, mesh=mesh, in_specs=placed, out_specs=P(("row", "col"), None), check_vma=False
    )
```
